768 devices in a mesh: space: 12 (over z), bal: 64 (over x, y, core).
Axes of the slice: x: 4, y: 8, z: 12, core: 2. Of those that a mesh axis runs over, the one named last changes fastest.
Arguments:
- panels: bfloat16 [12, 64, 1024, 1024], P('space', 'bal'), may hold values from -0.1875 to 0.1875
- enrich: int32 [12, 64], P('space', 'bal'), may hold values from 1 to 2
- compliance: float32 [12, 64, 1024], P('space', 'bal'), may hold values from 0.5 to 2
- loads: float32 [12, 64, 64, 1024], P('space', 'bal'), may hold values from -6 to 6
- face_maps: int32 [12, 64, 4, 256], P('space', 'bal'), may hold values from 0 to 255, each once within a row
- face_lengths: int32 [12, 64, 4], P('space', 'bal'), may hold values from 128 to 256, as said below
- contact: int32 [12, 64, 128], P('space', 'bal'), may hold values from 0 to 1023
Outputs:
- solution: float32 [12, 64, 64, 1024], P('space', 'bal')
- residual: float32 [12, 64, 64, 1024], P('space', 'bal')
- violation: float32 [64], replicated
The draws below stay inside these ranges and needn't reach their ends.
Inputs may be any that keep to these rules, and one draw needn't show every extreme that they name: `face_maps`: each face's slot-to-row table is a permutation of its 256 rows. `face_lengths`: the two faces of one shared interface have the same length; some face has all 256 slots live.
All inputs are finite; a program needn't handle non-finite values.
Results may differ from the reference program's by a relative error of at most 0.0003.
Values sent between devices are 32-bit elements; how exact they have to be, the bound alone decides.
No kernel may reach another device: no remote copies, remote signals or barrier semaphores. Data moves between devices by JAX's collectives and lax.ppermute only.
A program may use at most 32 MiB of HBM per device.

```python
import math
import jax
import jax.numpy as jnp
from jax import lax

IFACE = 1024
FACE = 256
ROWS = 1024
BLOCK_ROWS = 512
LOADS = 64
ITERS = 3
CONTACT = 128
SUB_S = 12
SUB_B = 64


def draw_face_lengths(key, part):
    first_key, second_key = jax.random.split(jax.random.fold_in(key, 11))
    shortest = FACE // 2
    space_len = jax.random.randint(first_key, (SUB_S + 1, SUB_B), shortest, FACE + 1).astype(jnp.int32)
    space_len = space_len.at[1, 0].set(FACE)
    bal_len = jax.random.randint(second_key, (SUB_S, SUB_B + 1), shortest, FACE + 1).astype(jnp.int32)
    stacked = jnp.stack([space_len[:-1], space_len[1:], bal_len[:, :-1], bal_len[:, 1:]], axis=2)
    return stacked.astype(jnp.int32)


def plant(drawn, rng, least, largest):
    extent = drawn.shape
    spot = [jax.random.randint(jax.random.fold_in(rng, axis), (), 0, extent[axis]) for axis in range(len(extent))]
    drawn = drawn.at[tuple(spot)].set(least)
    longest = extent.index(max(extent))
    spot[longest] = (spot[longest] + 1) % extent[longest]
    return drawn.at[tuple(spot)].set(largest)


def levels(rng, shape, pieces, low, top_value):
    def one(dim, parts):
        heights = jax.random.uniform(jax.random.fold_in(jax.random.fold_in(rng, 6), dim), (parts,), jnp.float32, low / len(pieces), top_value / len(pieces))
        return jnp.repeat(jnp.exp(heights), shape[dim] // parts).reshape((-1,) + (1,) * (len(shape) - dim - 1))

    gain = one(*pieces[0])
    for cut in pieces[1:]:
        gain = gain * one(*cut)
    return gain


def centred(stream_key, extent, scale, reach, pieces=(), kind=jnp.bfloat16):
    level = levels(stream_key, extent, pieces, -0.22, 0.18) if pieces else 1.0
    drawn = jax.random.normal(stream_key, extent, jnp.float32) * scale * level
    return jnp.minimum(jnp.maximum(drawn, -reach), reach).astype(kind)


def setup_inputs(seed: int = 0) -> dict:
    arg_keys = jax.random.split(jax.random.key(seed), 8)
    panels = centred(arg_keys[0], (SUB_S, SUB_B, ROWS, IFACE), ROWS ** -0.5, 0.1875, ((0, 12), (1, 64)))
    enrich = plant(jax.random.randint(arg_keys[1], (SUB_S, SUB_B), 1, ROWS // BLOCK_ROWS + 1), jax.random.fold_in(arg_keys[1], 1), 1, (ROWS // BLOCK_ROWS + 1) - 1).astype(jnp.int32)
    compliance = jnp.clip(jnp.exp(math.log(2.0) - 1.3862944 * jax.random.uniform(arg_keys[2], (SUB_S, SUB_B, IFACE), jnp.float32) ** levels(arg_keys[2], (SUB_S, SUB_B, IFACE), ((0, 12), (1, 64)), -0.2, 0.2)), 0.5, 2.0)
    loads = centred(arg_keys[3], (SUB_S, SUB_B, LOADS, IFACE), 1.0, 6.0, ((0, 12), (1, 64)), jnp.float32)
    face_maps = jax.vmap(lambda own: jax.random.permutation(own, FACE))(jax.random.split(arg_keys[4], SUB_S * SUB_B * 4)).reshape((SUB_S, SUB_B, 4, FACE)).astype(jnp.int32)
    face_lengths = draw_face_lengths(jax.random.fold_in(arg_keys[7], 71), 0)
    contact = plant(jax.random.randint(arg_keys[6], (SUB_S, SUB_B, CONTACT), 0, IFACE), jax.random.fold_in(arg_keys[6], 1), 0, IFACE - 1).astype(jnp.int32)
    return dict(panels=panels, enrich=enrich, compliance=compliance, loads=loads, face_maps=face_maps, face_lengths=face_lengths, contact=contact)


def chebyshev_constants():
    upper = 2.6 * (1.0 + math.sqrt(IFACE / ROWS)) ** 2 + 4.0
    lower = 0.5
    center = (upper + lower) / 2.0
    half_span = (upper - lower) / 2.0
    return (center, half_span, center / half_span)

def apply_local(direction, panels, enrich, compliance):
    row_index = jnp.arange(ROWS, dtype=jnp.int32)

    def one_sub(member):
        load_rows, panel_rows, live_blocks, diag_terms = member
        row_keep = (row_index < live_blocks * BLOCK_ROWS).astype(jnp.float32)
        kept = panel_rows.astype(jnp.float32) * row_keep[:, None]
        projected = jnp.dot(load_rows, kept.T, precision=lax.Precision.HIGHEST)
        return jnp.dot(projected, kept, precision=lax.Precision.HIGHEST) + load_rows * diag_terms[None, :]
    applied = lax.map(one_sub, (direction.reshape(-1, LOADS, IFACE), panels.reshape(-1, ROWS, IFACE), enrich.reshape(-1), compliance.reshape(-1, IFACE)))
    return applied.reshape(direction.shape)

def assemble_all(values, position, back_position):
    canonical = jnp.take_along_axis(values, jnp.broadcast_to(position, values.shape), axis=3)
    canonical = canonical.reshape(SUB_S, SUB_B, LOADS, 4, IFACE // 4)
    zero_space = jnp.zeros_like(canonical[:1, :, :, 0])
    zero_bal = jnp.zeros_like(canonical[:, :1, :, 0])
    from_below = jnp.concatenate([zero_space, canonical[:-1, :, :, 1]], axis=0)
    from_above = jnp.concatenate([canonical[1:, :, :, 0], zero_space], axis=0)
    from_left = jnp.concatenate([zero_bal, canonical[:, :-1, :, 3]], axis=1)
    from_right = jnp.concatenate([canonical[:, 1:, :, 2], zero_bal], axis=1)
    summed = canonical + jnp.stack([from_below, from_above, from_left, from_right], axis=3)
    summed = summed.reshape(values.shape)
    return jnp.take_along_axis(summed, jnp.broadcast_to(back_position, values.shape), axis=3)

def reference(panels, enrich, compliance, loads, face_maps, face_lengths, contact):
    face_len = IFACE // 4
    canon_slot = jnp.arange(face_len, dtype=jnp.int32)
    live_canon = (canon_slot[None, None, None, :] < face_lengths[:, :, :, None]).astype(jnp.float32)
    inverse = jnp.argsort(face_maps, axis=3).astype(jnp.int32)
    live_local = jnp.take_along_axis(live_canon, inverse, axis=3).reshape(SUB_S, SUB_B, 1, IFACE)
    offsets = (jnp.arange(4, dtype=jnp.int32) * face_len)[None, None, :, None]
    position = (face_maps + offsets).astype(jnp.int32).reshape(SUB_S, SUB_B, 1, IFACE)
    back_position = (inverse + offsets).astype(jnp.int32).reshape(SUB_S, SUB_B, 1, IFACE)
    center, half_span, ratio_c = chebyshev_constants()
    residual = assemble_all(live_local * loads, position, back_position)
    direction = residual / center
    solution = jnp.zeros_like(residual)
    cheb_rho = 1.0 / ratio_c
    for iteration in range(ITERS):
        solution = solution + direction
        image = live_local * apply_local(direction, panels, enrich, compliance)
        residual = residual - assemble_all(image, position, back_position)
        if iteration + 1 < ITERS:
            rho_next = 1.0 / (2.0 * ratio_c - cheb_rho)
            direction = rho_next * cheb_rho * direction + 2.0 * rho_next / half_span * residual
            cheb_rho = rho_next
    contact_index = jnp.broadcast_to(contact[:, :, None, :], (SUB_S, SUB_B, LOADS, CONTACT))
    gathered = jnp.take_along_axis(solution, contact_index, axis=3)
    negative = jnp.minimum(gathered, 0.0)
    violation = jnp.sqrt(lax.optimization_barrier(jnp.sum(negative * negative, axis=(0, 1, 3))) + 1e-06)
    return (solution, residual, violation)
```

```python
import functools
import math

import jax
import jax.numpy as jnp
from jax import lax
from jax.experimental import pallas as pl
from jax.experimental.pallas import tpu as pltpu
from jax.sharding import PartitionSpec as P

IFACE = 1024
FACE = 256
ROWS = 1024
BLOCK_ROWS = 512
LOADS = 64
ITERS = 3
CONTACT = 128
F32 = jnp.float32
BF16 = jnp.bfloat16
VM = pl.BlockSpec(memory_space=pltpu.VMEM)
SM = pl.BlockSpec(memory_space=pltpu.SMEM)
NN = (((1,), (0,)), ((), ()))
NT = (((1,), (1,)), ((), ()))


def chebyshev_constants():
    upper = 2.6 * (1.0 + math.sqrt(IFACE / ROWS)) ** 2 + 4.0
    lower = 0.5
    center = (upper + lower) / 2.0
    half_span = (upper - lower) / 2.0
    return (center, half_span, center / half_span)


def pieces(value, count):
    out = []
    for _ in range(count):
        piece = value.astype(BF16)
        out.append(piece)
        value = value - piece.astype(F32)
    return jnp.concatenate(out, axis=0)


def stacked_dot(value, matrix, dims, count):
    rows = value.shape[0]
    prod = lax.dot_general(pieces(value, count), matrix, dims, preferred_element_type=F32)
    total = prod[(count - 1) * rows :]
    for index in range(count - 2, -1, -1):
        total = total + prod[index * rows : (index + 1) * rows]
    return total


def one_hot(table_row):
    row = lax.broadcasted_iota(jnp.int32, (FACE, FACE), 0)
    return (row == table_row).astype(F32).astype(BF16)


def live_slots(lengths, face):
    slot = lax.broadcasted_iota(jnp.int32, (1, FACE), 1)
    return (slot < lengths[0, face]).astype(F32)


def loads_kernel(lengths, table, loads, perm, *sends):
    for face in range(4):
        hot = one_hot(table[face : face + 1, :])
        perm[face] = hot
        part = loads[:, face * FACE : (face + 1) * FACE]
        sends[face][...] = stacked_dot(part, hot, NN, 3) * live_slots(lengths, face)


def panel_kernel(enrich, panel, perm, compliance, contact, kept, diag, counts):
    live_rows = enrich[0, 0] * BLOCK_ROWS
    keep = lax.broadcasted_iota(jnp.int32, (ROWS, FACE), 0) < live_rows
    across = jnp.broadcast_to(contact[...], (CONTACT, CONTACT)).T
    for face in range(4):
        cols = slice(face * FACE, (face + 1) * FACE)
        moved = lax.dot_general(panel[:, cols], perm[face], NN, preferred_element_type=F32)
        kept[:, cols] = jnp.where(keep, moved, 0.0).astype(BF16)
        part = jnp.broadcast_to(compliance[:, cols], (8, FACE))
        diag[:, cols] = stacked_dot(part, perm[face], NN, 3)[0:1]
        tallies = []
        for half in range(FACE // CONTACT):
            base = face * FACE + half * CONTACT
            index = lax.broadcasted_iota(jnp.int32, (CONTACT, CONTACT), 1) + base
            tallies.append(jnp.sum((across == index).astype(F32), axis=0, keepdims=True))
        tally = jnp.broadcast_to(jnp.concatenate(tallies, axis=1), (8, FACE)).astype(BF16)
        counts[:, cols] = lax.dot_general(tally, perm[face], NN, preferred_element_type=F32)[0:1]


def step_kernel(first, last, keep_dir, add_res, lengths, kept, diag, *refs):
    own, got = refs[0:4], refs[4:8]
    refs = refs[8:]
    assembled = jnp.concatenate([o[...] + g[...] for o, g in zip(own, got)], axis=1)
    if first:
        residual = assembled
        direction = residual * add_res
        solution = direction
    else:
        residual = refs[0][...] - assembled
        direction = keep_dir * refs[1][...] + add_res * residual
        solution = refs[2][...] + direction
        refs = refs[3:]
    if last:
        counts, refs = refs[0], refs[1:]
    out_res, out_dir, out_sol = refs[0:3]
    sends = refs[3:7]
    out_res[...] = residual
    out_dir[...] = direction
    out_sol[...] = solution
    projected = stacked_dot(direction, kept[...], NT, 2)
    image = stacked_dot(projected, kept[...], NN, 2) + direction * diag[...]
    for face in range(4):
        cols = slice(face * FACE, (face + 1) * FACE)
        sends[face][...] = image[:, cols] * live_slots(lengths, face)
    if last:
        negative = jnp.minimum(solution, 0.0)
        weights = jnp.broadcast_to(counts[...], (8, IFACE)).astype(BF16)
        square = negative * negative
        terms = jnp.zeros((8, LOADS), F32)
        for _ in range(3):
            piece = square.astype(BF16)
            square = square - piece.astype(F32)
            terms = terms + lax.dot_general(weights, piece, NT, preferred_element_type=F32)
        refs[7][...] = jnp.broadcast_to(terms[0:1], refs[7].shape)


def solution_kernel(perm, field, out):
    for face in range(4):
        cols = slice(face * FACE, (face + 1) * FACE)
        out[:, cols] = stacked_dot(field[:, cols], perm[face], NT, 3)


def residual_kernel(perm, field, *refs):
    own, got, out = refs[0:4], refs[4:8], refs[8]
    for face in range(4):
        cols = slice(face * FACE, (face + 1) * FACE)
        value = field[:, cols] - (own[face][...] + got[face][...])
        out[:, cols] = stacked_dot(value, perm[face], NT, 3)


def call(body, name, out_shapes, in_specs):
    return pl.pallas_call(
        body,
        name=name,
        out_shape=[jax.ShapeDtypeStruct(shape, dtype) for shape, dtype in out_shapes],
        in_specs=in_specs,
        out_specs=[VM] * len(out_shapes),
    )


def exchange(sends):
    got = [None] * 4
    for axis, low in (("space", 0), ("bal", 2)):
        count = lax.axis_size(axis)
        forward = [(i, i + 1) for i in range(count - 1)]
        backward = [(target, source) for source, target in forward]
        got[low] = lax.ppermute(sends[low + 1], axis, forward)
        got[low + 1] = lax.ppermute(sends[low], axis, backward)
    return got


def total_over(row, axis):
    count = lax.axis_size(axis)
    spread = jnp.broadcast_to(row[None, :], (count, row.shape[0]))
    return jnp.sum(lax.all_to_all(spread, axis, 0, 0), axis=0)


def local(panels, enrich, compliance, loads, face_maps, face_lengths, contact):
    lengths = face_lengths.reshape(1, 4)
    center, half_span, ratio = chebyshev_constants()
    face_field = ((LOADS, FACE), F32)
    field = ((LOADS, IFACE), F32)
    perm, *sends = call(
        loads_kernel, "loads", [((4, FACE, FACE), BF16)] + [face_field] * 4, [SM, VM, VM]
    )(lengths, face_maps[0, 0], loads[0, 0])
    got = exchange(sends)
    kept, diag, counts = call(
        panel_kernel,
        "panel",
        [((ROWS, IFACE), BF16), ((1, IFACE), F32), ((1, IFACE), F32)],
        [SM, VM, VM, VM, VM],
    )(enrich, panels[0, 0], perm, compliance[0], contact[0])
    state = []
    rho = 1.0 / ratio
    keep_dir, add_res = 0.0, 1.0 / center
    for iteration in range(ITERS):
        last = iteration + 1 == ITERS
        inputs = [lengths, kept, diag, *sends, *got, *state] + ([counts] if last else [])
        outs = call(
            functools.partial(step_kernel, iteration == 0, last, keep_dir, add_res),
            "step",
            [field] * 3 + [face_field] * 4 + ([((8, LOADS), F32)] if last else []),
            [SM] + [VM] * (len(inputs) - 1),
        )(*inputs)
        state, sends = outs[0:3], outs[3:7]
        got = exchange(sends)
        rho_next = 1.0 / (2.0 * ratio - rho)
        keep_dir, add_res = rho_next * rho, 2.0 * rho_next / half_span
        rho = rho_next
    terms = outs[7][0]
    (solved,) = call(solution_kernel, "solved", [field], [VM, VM])(perm, state[2])
    (residual,) = call(residual_kernel, "residual", [field], [VM] * 10)(
        perm, state[0], *sends, *got
    )
    violation = jnp.sqrt(total_over(total_over(terms, "bal"), "space") + 1e-06)
    return (solved[None, None], residual[None, None], violation)


def solution(mesh):
    in_specs = (
        P("space", "bal", None, None),
        P("space", "bal"),
        P("space", "bal", None),
        P("space", "bal", None, None),
        P("space", "bal", None, None),
        P("space", "bal", None),
        P("space", "bal", None),
    )
    out_specs = (P("space", "bal", None, None), P("space", "bal", None, None), P())
    return jax.shard_map(local, mesh=mesh, in_specs=in_specs, out_specs=out_specs, check_vma=False)
```

```python
import functools
import math

import jax
import jax.numpy as jnp
from jax import lax
from jax.experimental import pallas as pl
from jax.experimental.pallas import tpu as pltpu
from jax.sharding import PartitionSpec as P


IFACE = 1024
FACE = 256
ROWS = 1024
BLOCK_ROWS = 512
LOADS = 64
ITERS = 3
CONTACT = 128
F32 = jnp.float32
BF16 = jnp.bfloat16
LIMIT = 20 * 1024 * 1024
VM = pl.BlockSpec(memory_space=pltpu.VMEM)
SM = pl.BlockSpec(memory_space=pltpu.SMEM)
HB = pl.BlockSpec(memory_space=pltpu.HBM)
CHUNKS = 4
NN = (((1,), (0,)), ((), ()))
NT = (((1,), (1,)), ((), ()))


def chebyshev_constants():
    upper = 2.6 * (1.0 + math.sqrt(IFACE / ROWS)) ** 2 + 4.0
    lower = 0.5
    center = (upper + lower) / 2.0
    half_span = (upper - lower) / 2.0
    return (center, half_span, center / half_span)


def pieces(value, count):
    out = []
    for _ in range(count):
        piece = value.astype(BF16)
        out.append(piece)
        value = value - piece.astype(F32)
    return jnp.concatenate(out, axis=0)


def stacked_dot(value, matrix, dims, count):
    rows = value.shape[0]
    prod = lax.dot_general(pieces(value, count), matrix, dims, preferred_element_type=F32)
    total = prod[(count - 1) * rows :]
    for index in range(count - 2, -1, -1):
        total = total + prod[index * rows : (index + 1) * rows]
    return total


def one_hot(table_row):
    row = lax.broadcasted_iota(jnp.int32, (FACE, FACE), 0)
    return (row == table_row).astype(F32).astype(BF16)


def fetch(pairs, sems):
    copies = []
    for index, (source, target) in enumerate(pairs):
        copies.append(pltpu.make_async_copy(source, target, sems.at[index]))
        copies[-1].start()
    return copies


def loads_kernel(lengths_hbm, table_hbm, loads_hbm, perm, live, *refs):
    sends, (lengths, table, loads, sems) = refs[0:4], refs[4:]
    pairs = [(lengths_hbm, lengths), (table_hbm, table), (loads_hbm, loads)]
    lengths_copy, table_copy, loads_copy = fetch(pairs, sems)
    lengths_copy.wait()
    slot = lax.broadcasted_iota(jnp.int32, (1, FACE), 1)
    for face in range(4):
        live[:, face * FACE : (face + 1) * FACE] = (slot < lengths[0, face]).astype(F32)
    table_copy.wait()
    hots = [one_hot(table[face : face + 1, :]) for face in range(4)]
    for face in range(4):
        perm[face] = hots[face]
    loads_copy.wait()
    for face in range(4):
        cols = slice(face * FACE, (face + 1) * FACE)
        sends[face][...] = stacked_dot(loads[:, cols], hots[face], NN, 3) * live[:, cols]


def panel_kernel(enrich, panel_hbm, diag_hbm, contact_hbm, perm, kept, diag, counts, *refs):
    panel, local_diag, contact, sems = refs
    height = ROWS // CHUNKS
    pairs = [(diag_hbm, local_diag), (contact_hbm, contact)]
    for chunk in range(CHUNKS):
        rows = pl.ds(chunk * height, height)
        pairs.append((panel_hbm.at[rows], panel.at[rows]))
    copies = fetch(pairs, sems)
    for copy in copies[0:2]:
        copy.wait()
    across = jnp.broadcast_to(contact[...], (CONTACT, CONTACT)).T
    for face in range(4):
        cols = slice(face * FACE, (face + 1) * FACE)
        part = jnp.broadcast_to(local_diag[:, cols], (8, FACE))
        diag[:, cols] = stacked_dot(part, perm[face], NN, 3)[0:1]
        tallies = []
        for half in range(FACE // CONTACT):
            base = face * FACE + half * CONTACT
            index = lax.broadcasted_iota(jnp.int32, (CONTACT, CONTACT), 1) + base
            tallies.append(jnp.sum((across == index).astype(F32), axis=0, keepdims=True))
        tally = jnp.broadcast_to(jnp.concatenate(tallies, axis=1), (8, FACE)).astype(BF16)
        counts[:, cols] = lax.dot_general(tally, perm[face], NN, preferred_element_type=F32)[0:1]
    for chunk in range(CHUNKS):
        rows = slice(chunk * height, (chunk + 1) * height)
        copies[2 + chunk].wait()
        block = chunk * height // BLOCK_ROWS

        @pl.when(block < enrich[0, 0])
        def _():
            for face in range(4):
                cols = slice(face * FACE, (face + 1) * FACE)
                moved = lax.dot_general(
                    panel[rows, cols], perm[face], NN, preferred_element_type=F32
                )
                kept[rows, cols] = moved.astype(BF16)

        @pl.when(block >= enrich[0, 0])
        def _():
            kept[rows, :] = jnp.zeros((height, IFACE), BF16)


def step_kernel(first, last, keep_dir, add_res, live, kept, diag, *refs):
    own, got = refs[0:4], refs[4:8]
    refs = refs[8:]
    assembled = jnp.concatenate([o[...] + g[...] for o, g in zip(own, got)], axis=1)
    if first:
        residual = assembled
        direction = residual * add_res
        solution = direction
    else:
        residual = refs[0][...] - assembled
        direction = keep_dir * refs[1][...] + add_res * residual
        solution = refs[2][...] + direction
        refs = refs[3:]
    if last:
        counts, refs = refs[0], refs[1:]
    out_res, out_dir, out_sol = refs[0:3]
    sends = refs[3:7]
    out_res[...] = residual
    out_dir[...] = direction
    out_sol[...] = solution
    projected = stacked_dot(direction, kept[...], NT, 2)
    image = stacked_dot(projected, kept[...], NN, 2) + direction * diag[...]
    for face in range(4):
        cols = slice(face * FACE, (face + 1) * FACE)
        sends[face][...] = image[:, cols] * live[:, cols]
    if last:
        negative = jnp.minimum(solution, 0.0)
        weights = jnp.broadcast_to(counts[...], (8, IFACE)).astype(BF16)
        square = negative * negative
        terms = jnp.zeros((8, LOADS), F32)
        for _ in range(3):
            piece = square.astype(BF16)
            square = square - piece.astype(F32)
            terms = terms + lax.dot_general(weights, piece, NT, preferred_element_type=F32)
        refs[7][...] = jnp.broadcast_to(terms[0:1][None], refs[7].shape)


def solution_kernel(perm, field, out):
    for face in range(4):
        cols = slice(face * FACE, (face + 1) * FACE)
        out[:, cols] = stacked_dot(field[:, cols], perm[face], NT, 3)


def residual_kernel(perm, field, *refs):
    own, got, out = refs[0:4], refs[4:8], refs[8]
    for face in range(4):
        cols = slice(face * FACE, (face + 1) * FACE)
        value = field[:, cols] - (own[face][...] + got[face][...])
        out[:, cols] = stacked_dot(value, perm[face], NT, 3)


def call(body, out_shapes, in_specs, scratch=()):
    return pl.pallas_call(
        body,
        out_shape=[jax.ShapeDtypeStruct(shape, dtype) for shape, dtype in out_shapes],
        in_specs=in_specs,
        scratch_shapes=scratch,
        out_specs=[VM] * len(out_shapes),
        compiler_params=pltpu.CompilerParams(vmem_limit_bytes=LIMIT),
    )


def in_hbm(array):
    return pltpu.with_memory_space_constraint(array, pltpu.HBM)


def exchange(sends):
    got = [None] * 4
    for axis, low in (("space", 0), ("bal", 2)):
        count = lax.axis_size(axis)
        forward = [(i, i + 1) for i in range(count - 1)]
        backward = [(target, source) for source, target in forward]
        got[low] = lax.ppermute(sends[low + 1], axis, forward)
        got[low + 1] = lax.ppermute(sends[low], axis, backward)
    return got


def local(panels, enrich, compliance, loads, face_maps, face_lengths, contact):
    center, half_span, ratio = chebyshev_constants()
    face_field = ((LOADS, FACE), F32)
    field = ((LOADS, IFACE), F32)
    flag = ((1, IFACE), F32)
    perm, live, *sends = call(
        loads_kernel,
        [((4, FACE, FACE), BF16), flag] + [face_field] * 4,
        [HB] * 3,
        [
            pltpu.SMEM((1, 4), jnp.int32),
            pltpu.VMEM((4, FACE), jnp.int32),
            pltpu.VMEM((LOADS, IFACE), F32),
            pltpu.SemaphoreType.DMA((3,)),
        ],
    )(in_hbm(face_lengths[0]), in_hbm(face_maps[0, 0]), in_hbm(loads[0, 0]))
    got = exchange(sends)
    kept, diag, counts = call(
        panel_kernel,
        [((ROWS, IFACE), BF16), flag, flag],
        [SM] + [HB] * 3 + [VM],
        [
            pltpu.VMEM((ROWS, IFACE), BF16),
            pltpu.VMEM((1, IFACE), F32),
            pltpu.VMEM((1, CONTACT), jnp.int32),
            pltpu.SemaphoreType.DMA((CHUNKS + 2,)),
        ],
    )(enrich, in_hbm(panels[0, 0]), in_hbm(compliance[0]), in_hbm(contact[0]), perm)
    state = []
    rho = 1.0 / ratio
    keep_dir, add_res = 0.0, 1.0 / center
    for iteration in range(ITERS):
        last = iteration + 1 == ITERS
        inputs = [live, kept, diag, *sends, *got, *state] + ([counts] if last else [])
        outs = call(
            functools.partial(step_kernel, iteration == 0, last, keep_dir, add_res),
            [field] * 3 + [face_field] * 4 + ([((lax.axis_size("bal"), 1, LOADS), F32)] if last else []),
            [VM] * len(inputs),
        )(*inputs)
        state, sends = outs[0:3], outs[3:7]
        got = exchange(sends)
        rho_next = 1.0 / (2.0 * ratio - rho)
        keep_dir, add_res = rho_next * rho, 2.0 * rho_next / half_span
        rho = rho_next
    heard = lax.all_to_all(outs[7], "bal", 0, 0)
    part = jnp.sum(heard, axis=0, keepdims=True)
    spread = jnp.broadcast_to(part, (lax.axis_size("space"), 1, LOADS))
    heard = lax.all_to_all(spread, "space", 0, 0)
    (solved,) = call(solution_kernel, [field], [VM, VM])(perm, state[2])
    (residual,) = call(residual_kernel, [field], [VM] * 10)(perm, state[0], *sends, *got)
    violation = jnp.sqrt(jnp.sum(heard[:, 0], axis=0) + 1e-06)
    return (solved[None, None], residual[None, None], violation)


def solution(mesh):
    in_specs = (
        P("space", "bal", None, None),
        P("space", "bal"),
        P("space", "bal", None),
        P("space", "bal", None, None),
        P("space", "bal", None, None),
        P("space", "bal", None),
        P("space", "bal", None),
    )
    out_specs = (P("space", "bal", None, None), P("space", "bal", None, None), P())

    return jax.shard_map(local, mesh=mesh, in_specs=in_specs, out_specs=out_specs, check_vma=False)
```
